128 devices in a mesh: sx: 4 (over x), sy: 2 (over z_hi), op: 16 (over y, z_lo, core).
Axes of the slice: x: 4, y: 4, z: 4 (z_hi: 2, z_lo: 2; z = z_hi * 2 + z_lo), core: 2. Of those that a mesh axis runs over, the one named last changes fastest.
Arguments:
- op_real: float32 [4, 2, 6144, 6144], P('sx', 'sy', 'op'), may hold values from -0.0546875 to 0.0546875
- op_imag: float32 [4, 2, 6144, 6144], P('sx', 'sy', 'op'), may hold values from -0.0546875 to 0.0546875
- coef_right: float32 [4, 2, 2, 6144], P('sx', 'sy', None, 'op'), may hold values from -3 to 3
- coef_upper: float32 [4, 2, 2, 6144], P('sx', 'sy', None, 'op'), may hold values from -3 to 3
- sources: float32 [4, 2, 2, 16, 6144], P('sx', 'sy', None, None, 'op'), may hold values from -6 to 6
Outputs:
- traces: float32 [4, 2, 2, 16, 6144], P('sx', 'sy', None, None, 'op')
The draws below stay inside these ranges and needn't reach their ends.
All inputs are finite; a program needn't handle non-finite values.
Results may differ from the reference program's by a relative error of at most 0.0003.
Values sent between devices are 32-bit elements; how exact they have to be, the bound alone decides.
No kernel may reach another device: no remote copies, remote signals or barrier semaphores. Data moves between devices by JAX's collectives and lax.ppermute only.
A program may use at most 64 MiB of HBM per device.

```python
import jax
import jax.numpy as jnp
from jax import lax

M = 6144
SRC = 16
NCOL = 4
NROW = 2


def block_levels(own_key, extent, pieces, low, top_value):
    level = 1.0
    for axis_at, blocks in pieces:
        steps = jax.random.uniform(jax.random.fold_in(jax.random.fold_in(own_key, 6), axis_at), (blocks,), jnp.float32, low / len(pieces), top_value / len(pieces))
        level = level * jnp.repeat(jnp.exp(steps), extent[axis_at] // blocks).reshape((-1,) + (1,) * (len(extent) - 1 - axis_at))
    return level


def bell_draw(rng, dims, scale, reach, cuts=(), held_as=jnp.bfloat16):
    values = jax.random.normal(rng, dims, jnp.float32) * scale
    if len(cuts) > 0:
        values = block_levels(rng, dims, cuts, -0.22, 0.18) * values
    return jnp.clip(values, min=-reach, max=reach).astype(held_as)


def setup_inputs(seed: int = 0) -> dict:
    key_list = jax.random.split(jax.random.key(seed), 6)
    return {
        "op_real": bell_draw(key_list[0], (NCOL, NROW, M, M), (2 * M) ** -0.5, 0.0546875, ((0, 4), (1, 2), (2, 16)), jnp.float32),
        "op_imag": bell_draw(key_list[1], (NCOL, NROW, M, M), (2 * M) ** -0.5, 0.0546875, ((0, 4), (1, 2), (2, 16)), jnp.float32),
        "coef_right": bell_draw(key_list[2], (NCOL, NROW, 2, M), 0.5, 3.0, ((0, 4), (1, 2), (3, 16)), jnp.float32),
        "coef_upper": bell_draw(key_list[3], (NCOL, NROW, 2, M), 0.5, 3.0, ((0, 4), (1, 2), (3, 16)), jnp.float32),
        "sources": bell_draw(key_list[4], (NCOL, NROW, 2, SRC, M), 1.0, 6.0, ((0, 4), (1, 2), (4, 16)), jnp.float32),
    }


def contract(left, right):
    return lax.dot_general(left, right, (((1,), (1,)), ((), ())), precision=lax.Precision.HIGHEST, preferred_element_type=jnp.float32)


def complex_scale(coef, field):
    real_part = coef[0][None, :] * field[0] - coef[1][None, :] * field[1]
    imag_part = coef[0][None, :] * field[1] + coef[1][None, :] * field[0]
    return jnp.stack([real_part, imag_part])


def apply_operator(real_mat, imag_mat, field):
    real_part = contract(field[0], real_mat) - contract(field[1], imag_mat)
    imag_part = contract(field[0], imag_mat) + contract(field[1], real_mat)
    return jnp.stack([real_part, imag_part])


def reference(op_real, op_imag, coef_right, coef_upper, sources):
    result = [[None] * NROW for column_at in range(NCOL)]
    for column_at in range(NCOL):
        for row_at in range(NROW):
            incoming = sources[column_at, row_at]
            if column_at > 0:
                incoming = incoming + complex_scale(coef_right[column_at, row_at], result[column_at - 1][row_at])
            if row_at > 0:
                incoming = incoming + complex_scale(coef_upper[column_at, row_at], result[column_at][row_at - 1])
            result[column_at][row_at] = apply_operator(op_real[column_at, row_at], op_imag[column_at, row_at], incoming)
    return jnp.stack([jnp.stack(column_list) for column_list in result])
```

```python
import functools

import jax
import jax.numpy as jnp
from jax import lax
from jax.experimental import pallas as pl
from jax.experimental.pallas import tpu as pltpu
from jax.sharding import Mesh
from jax.sharding import PartitionSpec as P

BF = jnp.bfloat16
F32 = jnp.float32
CHIPS = ("y", "zl")
VMEM_LIMIT = 12 * 1024 * 1024


def split(value):
    high = value.astype(BF)
    return high, (value - high.astype(F32)).astype(BF)


def prepare_body(
    fields_ref, real_hbm, imag_hbm, own_hi, own_lo, other_hi, other_lo, copies_ref, stage, sems
):
    rows, width = real_hbm.shape
    blocks = width // rows // 2
    which = lax.axis_index("core")

    def copies(at, slot):
        half, block = divmod(at, blocks)
        column = (2 * block + (which if half == 0 else 1 - which)) * rows
        column = pl.multiple_of(column, 128)
        return [
            pltpu.make_async_copy(ref.at[:, pl.ds(column, rows)], stage.at[slot, part], sems.at[slot, part])
            for part, ref in enumerate((real_hbm, imag_hbm))
        ]

    depth = stage.shape[0]
    for at in range(depth - 1):
        for copy in copies(at, at):
            copy.start()
    for at in range(2 * blocks):
        ahead = at + depth - 1
        if ahead < 2 * blocks:
            for copy in copies(ahead, ahead % depth):
                copy.start()
        for copy in copies(at, at % depth):
            copy.wait()
        half, block = divmod(at, blocks)
        hi_ref, lo_ref = ((own_hi, own_lo), (other_hi, other_lo))[half]
        for part in range(2):
            hi, lo = split(stage[at % depth, part])
            where = (pl.ds(block * rows, rows), pl.ds(part * rows, rows))
            hi_ref[where] = hi.T
            lo_ref[where] = lo.T
    for at in range(copies_ref.shape[0]):
        copies_ref[at] = fields_ref[...]


def prepare(fields, real_rows, imag_rows):
    rows, width = real_rows.shape
    half = pltpu.VMEM((width // 2, 2 * rows), BF)
    vmem = pl.BlockSpec(memory_space=pltpu.VMEM)
    return pl.pallas_call(
        prepare_body,
        in_specs=[
            vmem,
            pl.BlockSpec(memory_space=pltpu.HBM),
            pl.BlockSpec(memory_space=pltpu.HBM),
        ],
        out_specs=[vmem] * 5,
        out_shape=[half] * 4 + [jax.ShapeDtypeStruct((lax.axis_size(CHIPS), *fields.shape), F32)],
        scratch_shapes=[
            pltpu.VMEM((4, 2, rows, rows), F32),
            pltpu.SemaphoreType.DMA((4, 2)),
        ],
        compiler_params=pltpu.CompilerParams(vmem_limit_bytes=VMEM_LIMIT),
        cost_estimate=pl.CostEstimate(flops=0, transcendentals=0, bytes_accessed=8 * rows * width),
        name="prepare",
    )(
        fields,
        pltpu.with_memory_space_constraint(real_rows, pltpu.HBM),
        pltpu.with_memory_space_constraint(imag_rows, pltpu.HBM),
    )


def product(blocks_ref, hi_ref, lo_ref, xs):
    count, _, sources, rows = blocks_ref.shape
    for at in range(count):
        hi, lo = split(blocks_ref[at].reshape(2 * sources, rows))
        xs[: 2 * sources, pl.ds(at * rows, rows)] = hi
        xs[2 * sources :, pl.ds(at * rows, rows)] = lo
    dims = (((1,), (0,)), ((), ()))
    both = lax.dot_general(xs[...], hi_ref[...], dims, preferred_element_type=F32)
    rest = lax.dot_general(xs[: 2 * sources, :], lo_ref[...], dims, preferred_element_type=F32)
    return both[: 2 * sources] + both[2 * sources :] + rest


def diagonal():
    return lax.axis_index("sx") + lax.axis_index("sy")


def first_half_body(turn, blocks_ref, hi_ref, lo_ref, out_ref, xs):
    @pl.when(diagonal() == turn)
    def _():
        out_ref[...] = product(blocks_ref, hi_ref, lo_ref, xs)


def second_half_body(turn, blocks_ref, hi_ref, lo_ref, first_ref, before_ref, out_ref, xs):
    sources, rows = out_ref.shape[1:]

    @pl.when(diagonal() == turn)
    def _():
        total = first_ref[...] + product(blocks_ref, hi_ref, lo_ref, xs)
        with_real = total[:, :rows]
        with_imag = total[:, rows:]
        out_ref[0] = with_real[:sources] - with_imag[sources:]
        out_ref[1] = with_imag[:sources] + with_real[sources:]

    @pl.when(diagonal() != turn)
    def _():
        out_ref[...] = before_ref[...]


def half_call(body, turn, out_shape, blocks, *operands, name):
    vmem = pl.BlockSpec(memory_space=pltpu.VMEM)
    count, _, sources, rows = blocks.shape
    return pl.pallas_call(
        functools.partial(body, turn),
        in_specs=[vmem] * (1 + len(operands)),
        out_specs=vmem,
        out_shape=jax.ShapeDtypeStruct(out_shape, F32),
        scratch_shapes=[pltpu.VMEM((4 * sources, count * rows), BF)],
        compiler_params=pltpu.CompilerParams(vmem_limit_bytes=VMEM_LIMIT),
        name=name,
    )(blocks, *operands)


def scaled(coef, field):
    real_part = coef[0:1] * field[0] - coef[1:2] * field[1]
    imag_part = coef[0:1] * field[1] + coef[1:2] * field[0]
    return real_part, imag_part


def combine_body(fields_ref, right_ref, upper_ref, left_ref, below_ref, copies_ref):
    by_left = scaled(right_ref[...], left_ref[...])
    by_below = scaled(upper_ref[...], below_ref[...])
    for part in range(2):
        incoming = fields_ref[part] + by_left[part] + by_below[part]
        for at in range(copies_ref.shape[0]):
            copies_ref[at, part] = incoming


def combine(fields, right_coef, upper_coef, from_left, from_below):
    vmem = pl.BlockSpec(memory_space=pltpu.VMEM)
    return pl.pallas_call(
        combine_body,
        in_specs=[vmem] * 5,
        out_specs=vmem,
        out_shape=jax.ShapeDtypeStruct((lax.axis_size(CHIPS), *fields.shape), F32),
        compiler_params=pltpu.CompilerParams(vmem_limit_bytes=2 * 1024 * 1024),
        name="combine",
    )(fields, right_coef, upper_coef, from_left, from_below)


def ring(axis):
    size = lax.axis_size(axis)
    return [(i, (i + 1) % size) for i in range(size)]


def gather_chips(copies):
    return lax.all_to_all(copies, CHIPS, split_axis=0, concat_axis=0, tiled=True)


def hand_over(traces, turn, right, up):
    columns, rows = lax.axis_size("sx"), lax.axis_size("sy")
    pairs = []
    for column in range(columns):
        for row in range(rows):
            if column + row == turn and column + right < columns and row + up < rows:
                pairs.append((column * rows + row, (column + right) * rows + row + up))
    return lax.ppermute(traces, ("sx", "sy"), pairs)


def shards(op_real, op_imag, coef_right, coef_upper, sources):
    fields = sources[0, 0]
    _, count, rows = fields.shape
    right_coef = coef_right[0, 0]
    upper_coef = coef_upper[0, 0]
    rounds = lax.axis_size("sx") + lax.axis_size("sy") - 1
    *weights, copies = prepare(fields, op_real[0, 0], op_imag[0, 0])
    own_hi, own_lo, other_hi, other_lo = weights
    traces = fields
    for turn in range(rounds):
        if turn:
            from_left = hand_over(traces, turn - 1, 1, 0)
            from_below = hand_over(traces, turn - 1, 0, 1)
            copies = combine(fields, right_coef, upper_coef, from_left, from_below)
        own = gather_chips(copies)
        other = lax.ppermute(own, "core", ring("core"))
        first = half_call(
            first_half_body, turn, (2 * count, 2 * rows), own, own_hi, own_lo, name="first_half"
        )
        traces = half_call(
            second_half_body, turn, fields.shape, other, other_hi, other_lo, first, traces,
            name="second_half",
        )
    return traces[None, None]


def solution(mesh):
    fine = Mesh(mesh.devices.reshape(4, 2, 4, 2, 2), ("sx", "sy", "y", "zl", "core"))
    op = ("y", "zl", "core")
    return jax.shard_map(
        shards,
        mesh=fine,
        in_specs=(
            P("sx", "sy", op, None),
            P("sx", "sy", op, None),
            P("sx", "sy", None, op),
            P("sx", "sy", None, op),
            P("sx", "sy", None, None, op),
        ),
        out_specs=P("sx", "sy", None, None, op),
        check_vma=False,
    )
```

```python
import functools

import jax
import jax.numpy as jnp
from jax import lax
from jax.experimental import pallas as pl
from jax.experimental.pallas import tpu as pltpu
from jax.sharding import Mesh
from jax.sharding import PartitionSpec as P

BF = jnp.bfloat16
F32 = jnp.float32
CHIPS = ("y", "zl")
VMEM_LIMIT = 12 * 1024 * 1024


def split(value):
    high = value.astype(BF)
    return high, (value - high.astype(F32)).astype(BF)


def prepare_body(other, real_hbm, imag_hbm, *refs):
    hi_ref, lo_ref, stage, sems = refs[-4:]
    rows, width = real_hbm.shape
    blocks = width // rows // 2
    which = lax.axis_index("core")
    which = 1 - which if other else which

    def copies(block, slot):
        column = pl.multiple_of((2 * block + which) * rows, 128)
        return [
            pltpu.make_async_copy(ref.at[:, pl.ds(column, rows)], stage.at[slot, part], sems.at[slot, part])
            for part, ref in enumerate((real_hbm, imag_hbm))
        ]

    depth = stage.shape[0]
    for block in range(depth - 1):
        for copy in copies(block, block):
            copy.start()
    for block in range(blocks):
        ahead = block + depth - 1
        if ahead < blocks:
            for copy in copies(ahead, ahead % depth):
                copy.start()
        for copy in copies(block, block % depth):
            copy.wait()
        for part in range(2):
            hi, lo = split(stage[block % depth, part])
            where = (pl.ds(block * rows, rows), pl.ds(part * rows, rows))
            hi_ref[where] = hi.T
            lo_ref[where] = lo.T


def prepare(other, real_rows, imag_rows, *after):
    rows, width = real_rows.shape
    half = pltpu.VMEM((width // 2, 2 * rows), BF)
    return pl.pallas_call(
        functools.partial(prepare_body, other),
        in_specs=[
            pl.BlockSpec(memory_space=pltpu.HBM),
            pl.BlockSpec(memory_space=pltpu.HBM),
            *[pl.BlockSpec(memory_space=pltpu.VMEM)] * len(after),
        ],
        out_specs=[pl.BlockSpec(memory_space=pltpu.VMEM)] * 2,
        out_shape=[half] * 2,
        scratch_shapes=[
            pltpu.VMEM((4, 2, rows, rows), F32),
            pltpu.SemaphoreType.DMA((4, 2)),
        ],
        compiler_params=pltpu.CompilerParams(vmem_limit_bytes=VMEM_LIMIT),
        cost_estimate=pl.CostEstimate(flops=0, transcendentals=0, bytes_accessed=4 * rows * width),
        name="prepare_other" if other else "prepare_own",
    )(
        pltpu.with_memory_space_constraint(real_rows, pltpu.HBM),
        pltpu.with_memory_space_constraint(imag_rows, pltpu.HBM),
        *after,
    )


def relative(at):
    step, across = divmod(at, 2)
    count = lax.axis_size("y")
    y, zl = lax.axis_index("y"), lax.axis_index("zl")
    return 2 * ((y + count - step) % count) + (1 - zl if across else zl)


def product(turn, blocks_ref, hi_ref, lo_ref, xs):
    count, _, sources, rows = blocks_ref.shape
    for at in range(count):
        hi, lo = split(blocks_ref[at].reshape(2 * sources, rows))
        column = at * rows if turn else pl.multiple_of(relative(at) * rows, 128)
        xs[: 2 * sources, pl.ds(column, rows)] = hi
        xs[2 * sources :, pl.ds(column, rows)] = lo
    dims = (((1,), (0,)), ((), ()))
    both = lax.dot_general(xs[...], hi_ref[...], dims, preferred_element_type=F32)
    rest = lax.dot_general(xs[: 2 * sources, :], lo_ref[...], dims, preferred_element_type=F32)
    return both[: 2 * sources] + both[2 * sources :] + rest


def diagonal():
    return lax.axis_index("sx") + lax.axis_index("sy")


def first_half_body(turn, blocks_ref, hi_ref, lo_ref, out_ref, xs):
    @pl.when(diagonal() == turn)
    def _():
        out_ref[...] = product(turn, blocks_ref, hi_ref, lo_ref, xs)


def second_half_body(turn, blocks_ref, hi_ref, lo_ref, first_ref, before_ref, out_ref, xs):
    sources, rows = out_ref.shape[1:]

    @pl.when(diagonal() == turn)
    def _():
        total = first_ref[...] + product(turn, blocks_ref, hi_ref, lo_ref, xs)
        with_real = total[:, :rows]
        with_imag = total[:, rows:]
        out_ref[0] = with_real[:sources] - with_imag[sources:]
        out_ref[1] = with_imag[:sources] + with_real[sources:]

    @pl.when(diagonal() != turn)
    def _():
        out_ref[...] = before_ref[...]


def half_call(body, turn, out_shape, blocks, *operands, name):
    vmem = pl.BlockSpec(memory_space=pltpu.VMEM)
    count, _, sources, rows = blocks.shape
    return pl.pallas_call(
        functools.partial(body, turn),
        in_specs=[vmem] * (1 + len(operands)),
        out_specs=vmem,
        out_shape=jax.ShapeDtypeStruct(out_shape, F32),
        scratch_shapes=[pltpu.VMEM((4 * sources, count * rows), BF)],
        compiler_params=pltpu.CompilerParams(vmem_limit_bytes=VMEM_LIMIT),
        name=name,
    )(blocks, *operands)


def scaled(coef, field):
    real_part = coef[0:1] * field[0] - coef[1:2] * field[1]
    imag_part = coef[0:1] * field[1] + coef[1:2] * field[0]
    return real_part, imag_part


def combine_body(fields_ref, right_ref, upper_ref, left_ref, below_ref, copies_ref):
    by_left = scaled(right_ref[...], left_ref[...])
    by_below = scaled(upper_ref[...], below_ref[...])
    for part in range(2):
        incoming = fields_ref[part] + by_left[part] + by_below[part]
        for at in range(copies_ref.shape[0]):
            copies_ref[at, part] = incoming


def combine(fields, right_coef, upper_coef, from_left, from_below):
    vmem = pl.BlockSpec(memory_space=pltpu.VMEM)
    return pl.pallas_call(
        combine_body,
        in_specs=[vmem] * 5,
        out_specs=vmem,
        out_shape=jax.ShapeDtypeStruct((lax.axis_size(CHIPS), *fields.shape), F32),
        compiler_params=pltpu.CompilerParams(vmem_limit_bytes=2 * 1024 * 1024),
        name="combine",
    )(fields, right_coef, upper_coef, from_left, from_below)


def ring(axis):
    size = lax.axis_size(axis)
    return [(i, (i + 1) % size) for i in range(size)]


def gather_chips(copies):
    return lax.all_to_all(copies, CHIPS, split_axis=0, concat_axis=0, tiled=True)


def stack_body(count, *refs):
    out_ref = refs[-1]
    at = 0
    for ref in refs[:count]:
        for block in range(ref.shape[0]):
            out_ref[at] = ref[block]
            at += 1


def stack(blocks, after):
    total = sum(block.shape[0] for block in blocks)
    vmem = pl.BlockSpec(memory_space=pltpu.VMEM)
    return pl.pallas_call(
        functools.partial(stack_body, len(blocks)),
        in_specs=[vmem] * (len(blocks) + 1),
        out_specs=vmem,
        out_shape=jax.ShapeDtypeStruct((total, *blocks[0].shape[1:]), F32),
        compiler_params=pltpu.CompilerParams(vmem_limit_bytes=2 * 1024 * 1024),
        name="stack",
    )(*blocks, after)


def start(fields, real_rows, imag_rows):
    count = lax.axis_size("y")
    across = lax.ppermute(fields, "zl", ring("zl"))
    own_weights = prepare(False, real_rows, imag_rows)
    pair = stack([fields[None], across[None]], own_weights[0])
    others = [
        lax.ppermute(pair, "y", [(i, (i + step) % count) for i in range(count)])
        for step in range(1, count)
    ]
    other_weights = prepare(True, real_rows, imag_rows, pair)
    return stack([pair, *others], other_weights[0]), *own_weights, *other_weights


def hand_over(traces, turn, right, up):
    columns, rows = lax.axis_size("sx"), lax.axis_size("sy")
    pairs = []
    for column in range(columns):
        for row in range(rows):
            if column + row == turn and column + right < columns and row + up < rows:
                pairs.append((column * rows + row, (column + right) * rows + row + up))
    return lax.ppermute(traces, ("sx", "sy"), pairs)


def shards(op_real, op_imag, coef_right, coef_upper, sources):
    fields = sources[0, 0]
    _, count, rows = fields.shape
    right_coef = coef_right[0, 0]
    upper_coef = coef_upper[0, 0]
    rounds = lax.axis_size("sx") + lax.axis_size("sy") - 1
    own, own_hi, own_lo, other_hi, other_lo = start(fields, op_real[0, 0], op_imag[0, 0])
    traces = fields
    for turn in range(rounds):
        if turn:
            from_left = hand_over(traces, turn - 1, 1, 0)
            from_below = hand_over(traces, turn - 1, 0, 1)
            own = gather_chips(combine(fields, right_coef, upper_coef, from_left, from_below))
        other = lax.ppermute(own, "core", ring("core"))
        first = half_call(
            first_half_body, turn, (2 * count, 2 * rows), own, own_hi, own_lo, name="first_half"
        )
        traces = half_call(
            second_half_body, turn, fields.shape, other, other_hi, other_lo, first, traces,
            name="second_half",
        )
    return traces[None, None]


def solution(mesh):
    fine = Mesh(mesh.devices.reshape(4, 2, 4, 2, 2), ("sx", "sy", "y", "zl", "core"))
    op = ("y", "zl", "core")
    return jax.shard_map(
        shards,
        mesh=fine,
        in_specs=(
            P("sx", "sy", op, None),
            P("sx", "sy", op, None),
            P("sx", "sy", None, op),
            P("sx", "sy", None, op),
            P("sx", "sy", None, None, op),
        ),
        out_specs=P("sx", "sy", None, None, op),
        check_vma=False,
    )
```

```python
import functools

import jax
import jax.numpy as jnp
from jax import lax
from jax.experimental import pallas as pl
from jax.experimental.pallas import tpu as pltpu
from jax.sharding import Mesh
from jax.sharding import PartitionSpec as P

BF = jnp.bfloat16
F32 = jnp.float32
CHIPS = ("y", "zl")
CHUNK = 256
VMEM_LIMIT = 12 * 1024 * 1024


def split(value):
    high = value.astype(BF)
    return high, (value - high.astype(F32)).astype(BF)


def prepare_body(other, real_hbm, imag_hbm, *refs):
    hi_ref, lo_ref, stage, sems = refs[-4:]
    rows, width = real_hbm.shape
    blocks = width // rows // 2
    which = lax.axis_index("core")
    which = 1 - which if other else which

    def copies(block, slot):
        column = pl.multiple_of((2 * block + which) * rows, 128)
        return [
            pltpu.make_async_copy(ref.at[:, pl.ds(column, rows)], stage.at[slot, part], sems.at[slot, part])
            for part, ref in enumerate((real_hbm, imag_hbm))
        ]

    depth = stage.shape[0]
    for block in range(depth - 1):
        for copy in copies(block, block):
            copy.start()
    for block in range(blocks):
        ahead = block + depth - 1
        if ahead < blocks:
            for copy in copies(ahead, ahead % depth):
                copy.start()
        for copy in copies(block, block % depth):
            copy.wait()
        for part in range(2):
            hi, lo = split(stage[block % depth, part])
            where = (pl.ds(block * rows, rows), pl.ds(part * rows, rows))
            hi_ref[where] = hi.T
            lo_ref[where] = lo.T


def prepare(other, real_rows, imag_rows, *after):
    rows, width = real_rows.shape
    half = pltpu.VMEM((width // 2, 2 * rows), BF)
    return pl.pallas_call(
        functools.partial(prepare_body, other),
        in_specs=[
            pl.BlockSpec(memory_space=pltpu.HBM),
            pl.BlockSpec(memory_space=pltpu.HBM),
            *[pl.BlockSpec(memory_space=pltpu.VMEM)] * len(after),
        ],
        out_specs=[pl.BlockSpec(memory_space=pltpu.VMEM)] * 2,
        out_shape=[half] * 2,
        scratch_shapes=[
            pltpu.VMEM((8, 2, rows, rows), F32),
            pltpu.SemaphoreType.DMA((8, 2)),
        ],
        compiler_params=pltpu.CompilerParams(vmem_limit_bytes=VMEM_LIMIT),
        cost_estimate=pl.CostEstimate(flops=0, transcendentals=0, bytes_accessed=4 * rows * width),
        name="prepare_other" if other else "prepare_own",
    )(
        pltpu.with_memory_space_constraint(real_rows, pltpu.HBM),
        pltpu.with_memory_space_constraint(imag_rows, pltpu.HBM),
        *after,
    )


def relative(at):
    step, across = divmod(at, 2)
    count = lax.axis_size("y")
    y, zl = lax.axis_index("y"), lax.axis_index("zl")
    return 2 * ((y + count - step) % count) + (1 - zl if across else zl)


def product(turn, blocks_ref, hi_ref, lo_ref, xs):
    count, _, sources, rows = blocks_ref.shape
    for at in range(count):
        hi, lo = split(blocks_ref[at].reshape(2 * sources, rows))
        column = at * rows if turn else pl.multiple_of(relative(at) * rows, 128)
        xs[: 2 * sources, pl.ds(column, rows)] = hi
        xs[2 * sources :, pl.ds(column, rows)] = lo
    dims = (((1,), (0,)), ((), ()))
    total = None
    for at in range(0, count * rows, CHUNK):
        part = pl.ds(at, CHUNK)
        both = lax.dot_general(xs[:, part], hi_ref[part, :], dims, preferred_element_type=F32)
        rest = lax.dot_general(
            xs[: 2 * sources, part], lo_ref[part, :], dims, preferred_element_type=F32
        )
        both = both[: 2 * sources] + both[2 * sources :] + rest
        total = both if total is None else total + both
    return total


def diagonal():
    return lax.axis_index("sx") + lax.axis_index("sy")


def first_half_body(turn, blocks_ref, hi_ref, lo_ref, out_ref, xs):
    @pl.when(diagonal() == turn)
    def _():
        out_ref[...] = product(turn, blocks_ref, hi_ref, lo_ref, xs)


def second_half_body(turn, blocks_ref, hi_ref, lo_ref, first_ref, before_ref, out_ref, xs):
    sources, rows = out_ref.shape[1:]

    @pl.when(diagonal() == turn)
    def _():
        total = first_ref[...] + product(turn, blocks_ref, hi_ref, lo_ref, xs)
        with_real = total[:, :rows]
        with_imag = total[:, rows:]
        out_ref[0] = with_real[:sources] - with_imag[sources:]
        out_ref[1] = with_imag[:sources] + with_real[sources:]

    @pl.when(diagonal() != turn)
    def _():
        out_ref[...] = before_ref[...]


def half_call(body, turn, out_shape, blocks, *operands, name):
    vmem = pl.BlockSpec(memory_space=pltpu.VMEM)
    count, _, sources, rows = blocks.shape
    return pl.pallas_call(
        functools.partial(body, turn),
        in_specs=[vmem] * (1 + len(operands)),
        out_specs=vmem,
        out_shape=jax.ShapeDtypeStruct(out_shape, F32),
        scratch_shapes=[pltpu.VMEM((4 * sources, count * rows), BF)],
        compiler_params=pltpu.CompilerParams(vmem_limit_bytes=VMEM_LIMIT),
        name=name,
    )(blocks, *operands)


def scaled(coef, field):
    real_part = coef[0:1] * field[0] - coef[1:2] * field[1]
    imag_part = coef[0:1] * field[1] + coef[1:2] * field[0]
    return real_part, imag_part


def combine_body(fields_ref, right_ref, upper_ref, left_ref, below_ref, copies_ref):
    by_left = scaled(jnp.where(lax.axis_index("sx") > 0, right_ref[...], 0.0), left_ref[...])
    by_below = scaled(jnp.where(lax.axis_index("sy") > 0, upper_ref[...], 0.0), below_ref[...])
    for part in range(2):
        incoming = fields_ref[part] + by_left[part] + by_below[part]
        for at in range(copies_ref.shape[0]):
            copies_ref[at, part] = incoming


def combine(fields, right_coef, upper_coef, from_left, from_below):
    vmem = pl.BlockSpec(memory_space=pltpu.VMEM)
    return pl.pallas_call(
        combine_body,
        in_specs=[vmem] * 5,
        out_specs=vmem,
        out_shape=jax.ShapeDtypeStruct((lax.axis_size(CHIPS), *fields.shape), F32),
        compiler_params=pltpu.CompilerParams(vmem_limit_bytes=2 * 1024 * 1024),
        name="combine",
    )(fields, right_coef, upper_coef, from_left, from_below)


def ring(axis):
    size = lax.axis_size(axis)
    return [(i, (i + 1) % size) for i in range(size)]


def gather_chips(copies):
    return lax.all_to_all(copies, CHIPS, split_axis=0, concat_axis=0, tiled=True)


def stack_body(count, *refs):
    out_ref = refs[-1]
    at = 0
    for ref in refs[:count]:
        for block in range(ref.shape[0]):
            out_ref[at] = ref[block]
            at += 1


def stack(blocks, after):
    total = sum(block.shape[0] for block in blocks)
    vmem = pl.BlockSpec(memory_space=pltpu.VMEM)
    return pl.pallas_call(
        functools.partial(stack_body, len(blocks)),
        in_specs=[vmem] * (len(blocks) + 1),
        out_specs=vmem,
        out_shape=jax.ShapeDtypeStruct((total, *blocks[0].shape[1:]), F32),
        compiler_params=pltpu.CompilerParams(vmem_limit_bytes=2 * 1024 * 1024),
        name="stack",
    )(*blocks, after)


def start(fields, real_rows, imag_rows):
    count = lax.axis_size("y")
    across = lax.ppermute(fields, "zl", ring("zl"))
    own_weights = prepare(False, real_rows, imag_rows)
    pair = stack([fields[None], across[None]], own_weights[0])
    others = [
        lax.ppermute(pair, "y", [(i, (i + step) % count) for i in range(count)])
        for step in range(1, count)
    ]
    other_weights = prepare(True, real_rows, imag_rows, pair)
    return stack([pair, *others], other_weights[0]), *own_weights, *other_weights


def hand_over(traces, turn, right, up):
    columns, rows, cores = (lax.axis_size(name) for name in ("sx", "sy", "core"))
    windows = [(column, row) for column in range(columns) for row in range(rows)]
    target = {}
    for column, row in windows:
        there = (column + right, row + up)
        if column + row == turn and there in windows:
            target[column, row] = there
            if up:
                target[there] = (column, row)

    def index(window, core):
        return (window[0] * rows + window[1]) * cores + core

    pairs = []
    for window in windows:
        for core in range(cores):
            if window in target:
                pairs.append((index(window, core), index(target[window], core)))
            elif up:
                pairs.append((index(window, core), index(window, (core + 1) % cores)))
    return lax.ppermute(traces, ("sx", "sy", "core"), pairs)


def shards(op_real, op_imag, coef_right, coef_upper, sources):
    fields = sources[0, 0]
    _, count, rows = fields.shape
    right_coef = coef_right[0, 0]
    upper_coef = coef_upper[0, 0]
    rounds = lax.axis_size("sx") + lax.axis_size("sy") - 1
    own, own_hi, own_lo, other_hi, other_lo = start(fields, op_real[0, 0], op_imag[0, 0])
    traces = fields
    for turn in range(rounds):
        if turn:
            from_left = hand_over(traces, turn - 1, 1, 0)
            from_below = hand_over(traces, turn - 1, 0, 1)
            own = gather_chips(combine(fields, right_coef, upper_coef, from_left, from_below))
        other = lax.ppermute(own, "core", ring("core"))
        first = half_call(
            first_half_body, turn, (2 * count, 2 * rows), own, own_hi, own_lo, name="first_half"
        )
        traces = half_call(
            second_half_body, turn, fields.shape, other, other_hi, other_lo, first, traces,
            name="second_half",
        )
    return traces[None, None]


def solution(mesh):
    fine = Mesh(mesh.devices.reshape(4, 2, 4, 2, 2), ("sx", "sy", "y", "zl", "core"))
    op = ("y", "zl", "core")
    return jax.shard_map(
        shards,
        mesh=fine,
        in_specs=(
            P("sx", "sy", op, None),
            P("sx", "sy", op, None),
            P("sx", "sy", None, op),
            P("sx", "sy", None, op),
            P("sx", "sy", None, None, op),
        ),
        out_specs=P("sx", "sy", None, None, op),
        check_vma=False,
    )
```

```python
import functools

import jax
import jax.numpy as jnp
from jax import lax
from jax.experimental import pallas as pl
from jax.experimental.pallas import tpu as pltpu
from jax.sharding import Mesh
from jax.sharding import PartitionSpec as P

BF = jnp.bfloat16
F32 = jnp.float32
CHIPS = ("y", "zl")
CHUNK = 256
VMEM_LIMIT = 12 * 1024 * 1024


def split(value):
    high = value.astype(BF)
    return high, (value - high.astype(F32)).astype(BF)


def prepare_body(other, real_hbm, imag_hbm, *refs):
    hi_ref, lo_ref, stage, sems = refs[-4:]
    rows, width = real_hbm.shape
    blocks = width // rows // 2
    which = lax.axis_index("core")
    which = 1 - which if other else which

    def copies(block, slot):
        column = pl.multiple_of((2 * block + which) * rows, 128)
        return [
            pltpu.make_async_copy(ref.at[:, pl.ds(column, rows)], stage.at[slot, part], sems.at[slot, part])
            for part, ref in enumerate((real_hbm, imag_hbm))
        ]

    depth = stage.shape[0]
    for block in range(depth - 1):
        for copy in copies(block, block):
            copy.start()
    for block in range(blocks):
        ahead = block + depth - 1
        if ahead < blocks:
            for copy in copies(ahead, ahead % depth):
                copy.start()
        for copy in copies(block, block % depth):
            copy.wait()
        for part in range(2):
            where = (pl.ds(block * rows, rows), pl.ds(part * rows, rows))
            hi_ref[where], lo_ref[where] = split(stage[block % depth, part].T)


def prepare(other, real_rows, imag_rows, *after):
    rows, width = real_rows.shape
    half = pltpu.VMEM((width // 2, 2 * rows), BF)
    return pl.pallas_call(
        functools.partial(prepare_body, other),
        in_specs=[
            pl.BlockSpec(memory_space=pltpu.HBM),
            pl.BlockSpec(memory_space=pltpu.HBM),
            *[pl.BlockSpec(memory_space=pltpu.VMEM)] * len(after),
        ],
        out_specs=[pl.BlockSpec(memory_space=pltpu.VMEM)] * 2,
        out_shape=[half] * 2,
        scratch_shapes=[
            pltpu.VMEM((8, 2, rows, rows), F32),
            pltpu.SemaphoreType.DMA((8, 2)),
        ],
        compiler_params=pltpu.CompilerParams(vmem_limit_bytes=VMEM_LIMIT),
        cost_estimate=pl.CostEstimate(flops=0, transcendentals=0, bytes_accessed=4 * rows * width),
        name="prepare_other" if other else "prepare_own",
    )(
        pltpu.with_memory_space_constraint(real_rows, pltpu.HBM),
        pltpu.with_memory_space_constraint(imag_rows, pltpu.HBM),
        *after,
    )


def relative(at):
    step, across = divmod(at, 2)
    step = (0, 1, 3, 2)[step]
    count = lax.axis_size("y")
    y, zl = lax.axis_index("y"), lax.axis_index("zl")
    return 2 * ((y + count - step) % count) + (1 - zl if across else zl)


def product(turn, blocks_ref, hi_ref, lo_ref, xs):
    count, _, sources, rows = blocks_ref.shape
    for at in range(count):
        hi, lo = split(blocks_ref[at].reshape(2 * sources, rows))
        column = at * rows if turn else pl.multiple_of(relative(at) * rows, 128)
        xs[: 2 * sources, pl.ds(column, rows)] = hi
        xs[2 * sources :, pl.ds(column, rows)] = lo
    dims = (((1,), (0,)), ((), ()))
    total = None
    for at in range(0, count * rows, CHUNK):
        part = pl.ds(at, CHUNK)
        both = lax.dot_general(xs[:, part], hi_ref[part, :], dims, preferred_element_type=F32)
        rest = lax.dot_general(
            xs[: 2 * sources, part], lo_ref[part, :], dims, preferred_element_type=F32
        )
        both = both[: 2 * sources] + both[2 * sources :] + rest
        total = both if total is None else total + both
    return total


def diagonal():
    return lax.axis_index("sx") + lax.axis_index("sy")


def first_half_body(turn, blocks_ref, hi_ref, lo_ref, out_ref, xs):
    @pl.when(diagonal() == turn)
    def _():
        out_ref[...] = product(turn, blocks_ref, hi_ref, lo_ref, xs)


def second_half_body(turn, blocks_ref, hi_ref, lo_ref, first_ref, before_ref, out_ref, xs):
    sources, rows = out_ref.shape[1:]

    @pl.when(diagonal() == turn)
    def _():
        total = first_ref[...] + product(turn, blocks_ref, hi_ref, lo_ref, xs)
        with_real = total[:, :rows]
        with_imag = total[:, rows:]
        out_ref[0] = with_real[:sources] - with_imag[sources:]
        out_ref[1] = with_imag[:sources] + with_real[sources:]

    @pl.when(diagonal() != turn)
    def _():
        out_ref[...] = before_ref[...]


def half_call(body, turn, out_shape, blocks, *operands, name):
    vmem = pl.BlockSpec(memory_space=pltpu.VMEM)
    count, _, sources, rows = blocks.shape
    return pl.pallas_call(
        functools.partial(body, turn),
        in_specs=[vmem] * (1 + len(operands)),
        out_specs=vmem,
        out_shape=jax.ShapeDtypeStruct(out_shape, F32),
        scratch_shapes=[pltpu.VMEM((4 * sources, count * rows), BF)],
        compiler_params=pltpu.CompilerParams(vmem_limit_bytes=VMEM_LIMIT),
        name=name,
    )(blocks, *operands)


def scaled(coef, field):
    real_part = coef[0:1] * field[0] - coef[1:2] * field[1]
    imag_part = coef[0:1] * field[1] + coef[1:2] * field[0]
    return real_part, imag_part


def combine_body(fields_ref, right_ref, upper_ref, left_ref, below_ref, copies_ref):
    by_left = scaled(jnp.where(lax.axis_index("sx") > 0, right_ref[...], 0.0), left_ref[...])
    by_below = scaled(jnp.where(lax.axis_index("sy") > 0, upper_ref[...], 0.0), below_ref[...])
    for part in range(2):
        incoming = fields_ref[part] + by_left[part] + by_below[part]
        for at in range(copies_ref.shape[0]):
            copies_ref[at, part] = incoming


def combine(fields, right_coef, upper_coef, from_left, from_below):
    vmem = pl.BlockSpec(memory_space=pltpu.VMEM)
    return pl.pallas_call(
        combine_body,
        in_specs=[vmem] * 5,
        out_specs=vmem,
        out_shape=jax.ShapeDtypeStruct((lax.axis_size(CHIPS), *fields.shape), F32),
        compiler_params=pltpu.CompilerParams(vmem_limit_bytes=2 * 1024 * 1024),
        name="combine",
    )(fields, right_coef, upper_coef, from_left, from_below)


def ring(axis):
    size = lax.axis_size(axis)
    return [(i, (i + 1) % size) for i in range(size)]


def gather_chips(copies):
    return lax.all_to_all(copies, CHIPS, split_axis=0, concat_axis=0, tiled=True)


def stack_body(count, *refs):
    out_ref = refs[-1]
    at = 0
    for ref in refs[:count]:
        for block in range(ref.shape[0]):
            out_ref[at] = ref[block]
            at += 1


def stack(blocks, after):
    total = sum(block.shape[0] for block in blocks)
    vmem = pl.BlockSpec(memory_space=pltpu.VMEM)
    return pl.pallas_call(
        functools.partial(stack_body, len(blocks)),
        in_specs=[vmem] * (len(blocks) + 1),
        out_specs=vmem,
        out_shape=jax.ShapeDtypeStruct((total, *blocks[0].shape[1:]), F32),
        compiler_params=pltpu.CompilerParams(vmem_limit_bytes=2 * 1024 * 1024),
        name="stack",
    )(*blocks, after)


def start(fields, real_rows, imag_rows):
    count = lax.axis_size("y")
    across = lax.ppermute(fields, "zl", ring("zl"))
    own_weights = prepare(False, real_rows, imag_rows)
    pair = stack([fields[None], across[None]], own_weights[0])
    others = [
        lax.ppermute(pair, "y", [(i, (i + step) % count) for i in range(count)])
        for step in (1, 3, 2)
    ]
    other_weights = prepare(True, real_rows, imag_rows, pair)
    return stack([pair, *others], other_weights[0]), *own_weights, *other_weights


def hand_over(traces, turn, right, up):
    columns, rows, cores = (lax.axis_size(name) for name in ("sx", "sy", "core"))
    windows = [(column, row) for column in range(columns) for row in range(rows)]
    target = {}
    for column, row in windows:
        there = (column + right, row + up)
        if column + row == turn and there in windows:
            target[column, row] = there
            if up:
                target[there] = (column, row)

    def index(window, core):
        return (window[0] * rows + window[1]) * cores + core

    pairs = []
    for window in windows:
        for core in range(cores):
            if window in target:
                pairs.append((index(window, core), index(target[window], core)))
            elif up:
                pairs.append((index(window, core), index(window, (core + 1) % cores)))
    return lax.ppermute(traces, ("sx", "sy", "core"), pairs)


def shards(op_real, op_imag, coef_right, coef_upper, sources):
    fields = sources[0, 0]
    _, count, rows = fields.shape
    right_coef = coef_right[0, 0]
    upper_coef = coef_upper[0, 0]
    rounds = lax.axis_size("sx") + lax.axis_size("sy") - 1
    own, own_hi, own_lo, other_hi, other_lo = start(fields, op_real[0, 0], op_imag[0, 0])
    traces = fields
    for turn in range(rounds):
        if turn:
            from_left = hand_over(traces, turn - 1, 1, 0)
            from_below = hand_over(traces, turn - 1, 0, 1)
            own = gather_chips(combine(fields, right_coef, upper_coef, from_left, from_below))
        other = lax.ppermute(own, "core", ring("core"))
        first = half_call(
            first_half_body, turn, (2 * count, 2 * rows), own, own_hi, own_lo, name="first_half"
        )
        traces = half_call(
            second_half_body, turn, fields.shape, other, other_hi, other_lo, first, traces,
            name="second_half",
        )
    return traces[None, None]


def solution(mesh):
    fine = Mesh(mesh.devices.reshape(4, 2, 4, 2, 2), ("sx", "sy", "y", "zl", "core"))
    op = ("y", "zl", "core")
    return jax.shard_map(
        shards,
        mesh=fine,
        in_specs=(
            P("sx", "sy", op, None),
            P("sx", "sy", op, None),
            P("sx", "sy", None, op),
            P("sx", "sy", None, op),
            P("sx", "sy", None, None, op),
        ),
        out_specs=P("sx", "sy", None, None, op),
        check_vma=False,
    )
```

```python
import functools

import jax
import jax.numpy as jnp
from jax import lax
from jax.experimental import pallas as pl
from jax.experimental.pallas import tpu as pltpu
from jax.sharding import Mesh
from jax.sharding import PartitionSpec as P

BF = jnp.bfloat16
F32 = jnp.float32
CHIPS = ("y", "zl")
CHUNK = 256
VMEM_LIMIT = 12 * 1024 * 1024


def split(value):
    high = value.astype(BF)
    return high, (value - high.astype(F32)).astype(BF)


def prepare_body(other, real_hbm, imag_hbm, *refs):
    hi_ref, lo_ref, stage, sems = refs[-4:]
    rows, width = real_hbm.shape
    blocks = width // rows // 2
    which = lax.axis_index("core")
    which = 1 - which if other else which

    def copies(block, slot):
        column = pl.multiple_of((2 * block + which) * rows, 128)
        return [
            pltpu.make_async_copy(ref.at[:, pl.ds(column, rows)], stage.at[slot, part], sems.at[slot, part])
            for part, ref in enumerate((real_hbm, imag_hbm))
        ]

    depth = stage.shape[0]
    for block in range(depth - 1):
        for copy in copies(block, block):
            copy.start()
    for block in range(blocks):
        ahead = block + depth - 1
        if ahead < blocks:
            for copy in copies(ahead, ahead % depth):
                copy.start()
        arriving = copies(block, block % depth)
        for part in range(2):
            arriving[part].wait()
            where = (pl.ds(block * rows, rows), pl.ds(part * rows, rows))
            hi_ref[where], lo_ref[where] = split(stage[block % depth, part].T)


def prepare(other, real_rows, imag_rows, *after):
    rows, width = real_rows.shape
    half = pltpu.VMEM((width // 2, 2 * rows), BF)
    return pl.pallas_call(
        functools.partial(prepare_body, other),
        in_specs=[
            pl.BlockSpec(memory_space=pltpu.HBM),
            pl.BlockSpec(memory_space=pltpu.HBM),
            *[pl.BlockSpec(memory_space=pltpu.VMEM)] * len(after),
        ],
        out_specs=[pl.BlockSpec(memory_space=pltpu.VMEM)] * 2,
        out_shape=[half] * 2,
        scratch_shapes=[
            pltpu.VMEM((8, 2, rows, rows), F32),
            pltpu.SemaphoreType.DMA((8, 2)),
        ],
        compiler_params=pltpu.CompilerParams(vmem_limit_bytes=VMEM_LIMIT),
        cost_estimate=pl.CostEstimate(flops=0, transcendentals=0, bytes_accessed=4 * rows * width),
        name="prepare_other" if other else "prepare_own",
    )(
        pltpu.with_memory_space_constraint(real_rows, pltpu.HBM),
        pltpu.with_memory_space_constraint(imag_rows, pltpu.HBM),
        *after,
    )


def relative(at):
    step, across = divmod(at, 2)
    step = (0, 1, 3, 2)[step]
    count = lax.axis_size("y")
    y, zl = lax.axis_index("y"), lax.axis_index("zl")
    return 2 * ((y + count - step) % count) + (1 - zl if across else zl)


def product(turn, blocks_ref, hi_ref, lo_ref, xs):
    count, _, sources, rows = blocks_ref.shape
    for at in range(count):
        hi, lo = split(blocks_ref[at].reshape(2 * sources, rows))
        column = at * rows if turn else pl.multiple_of(relative(at) * rows, 128)
        xs[: 2 * sources, pl.ds(column, rows)] = hi
        xs[2 * sources :, pl.ds(column, rows)] = lo
    dims = (((1,), (0,)), ((), ()))
    total = None
    for at in range(0, count * rows, CHUNK):
        part = pl.ds(at, CHUNK)
        both = lax.dot_general(xs[:, part], hi_ref[part, :], dims, preferred_element_type=F32)
        rest = lax.dot_general(
            xs[: 2 * sources, part], lo_ref[part, :], dims, preferred_element_type=F32
        )
        both = both[: 2 * sources] + both[2 * sources :] + rest
        total = both if total is None else total + both
    return total


def diagonal():
    return lax.axis_index("sx") + lax.axis_index("sy")


def first_half_body(turn, blocks_ref, hi_ref, lo_ref, out_ref, xs):
    @pl.when(diagonal() == turn)
    def _():
        out_ref[...] = product(turn, blocks_ref, hi_ref, lo_ref, xs)


def second_half_body(turn, blocks_ref, hi_ref, lo_ref, first_ref, before_ref, out_ref, xs):
    sources, rows = out_ref.shape[1:]

    @pl.when(diagonal() == turn)
    def _():
        total = first_ref[...] + product(turn, blocks_ref, hi_ref, lo_ref, xs)
        with_real = total[:, :rows]
        with_imag = total[:, rows:]
        out_ref[0] = with_real[:sources] - with_imag[sources:]
        out_ref[1] = with_imag[:sources] + with_real[sources:]

    @pl.when(diagonal() != turn)
    def _():
        out_ref[...] = before_ref[...]


def half_call(body, turn, out_shape, blocks, *operands, name):
    vmem = pl.BlockSpec(memory_space=pltpu.VMEM)
    count, _, sources, rows = blocks.shape
    return pl.pallas_call(
        functools.partial(body, turn),
        in_specs=[vmem] * (1 + len(operands)),
        out_specs=vmem,
        out_shape=jax.ShapeDtypeStruct(out_shape, F32),
        scratch_shapes=[pltpu.VMEM((4 * sources, count * rows), BF)],
        compiler_params=pltpu.CompilerParams(vmem_limit_bytes=VMEM_LIMIT),
        name=name,
    )(blocks, *operands)


def scaled(coef, field):
    real_part = coef[0:1] * field[0] - coef[1:2] * field[1]
    imag_part = coef[0:1] * field[1] + coef[1:2] * field[0]
    return real_part, imag_part


def combine_body(fields_ref, right_ref, upper_ref, left_ref, below_ref, copies_ref):
    by_left = scaled(jnp.where(lax.axis_index("sx") > 0, right_ref[...], 0.0), left_ref[...])
    by_below = scaled(jnp.where(lax.axis_index("sy") > 0, upper_ref[...], 0.0), below_ref[...])
    for part in range(2):
        incoming = fields_ref[part] + by_left[part] + by_below[part]
        for at in range(copies_ref.shape[0]):
            copies_ref[at, part] = incoming


def combine(fields, right_coef, upper_coef, from_left, from_below):
    vmem = pl.BlockSpec(memory_space=pltpu.VMEM)
    return pl.pallas_call(
        combine_body,
        in_specs=[vmem] * 5,
        out_specs=vmem,
        out_shape=jax.ShapeDtypeStruct((lax.axis_size(CHIPS), *fields.shape), F32),
        compiler_params=pltpu.CompilerParams(vmem_limit_bytes=2 * 1024 * 1024),
        name="combine",
    )(fields, right_coef, upper_coef, from_left, from_below)


def ring(axis):
    size = lax.axis_size(axis)
    return [(i, (i + 1) % size) for i in range(size)]


def gather_chips(copies):
    return lax.all_to_all(copies, CHIPS, split_axis=0, concat_axis=0, tiled=True)


def stack_body(count, *refs):
    out_ref = refs[-1]
    at = 0
    for ref in refs[:count]:
        for block in range(ref.shape[0]):
            out_ref[at] = ref[block]
            at += 1


def stack(blocks, after):
    total = sum(block.shape[0] for block in blocks)
    vmem = pl.BlockSpec(memory_space=pltpu.VMEM)
    return pl.pallas_call(
        functools.partial(stack_body, len(blocks)),
        in_specs=[vmem] * (len(blocks) + 1),
        out_specs=vmem,
        out_shape=jax.ShapeDtypeStruct((total, *blocks[0].shape[1:]), F32),
        compiler_params=pltpu.CompilerParams(vmem_limit_bytes=2 * 1024 * 1024),
        name="stack",
    )(*blocks, after)


def start(fields, real_rows, imag_rows):
    count = lax.axis_size("y")
    across = lax.ppermute(fields, "zl", ring("zl"))
    own_weights = prepare(False, real_rows, imag_rows)
    pair = stack([fields[None], across[None]], own_weights[0])
    others = [
        lax.ppermute(pair, "y", [(i, (i + step) % count) for i in range(count)])
        for step in (1, 3, 2)
    ]
    other_weights = prepare(True, real_rows, imag_rows, pair)
    return stack([pair, *others], other_weights[0]), *own_weights, *other_weights


def hand_over(traces, turn, right, up):
    columns, rows, cores = (lax.axis_size(name) for name in ("sx", "sy", "core"))
    windows = [(column, row) for column in range(columns) for row in range(rows)]
    target = {}
    for column, row in windows:
        there = (column + right, row + up)
        if column + row == turn and there in windows:
            target[column, row] = there
            if up:
                target[there] = (column, row)

    def index(window, core):
        return (window[0] * rows + window[1]) * cores + core

    pairs = []
    for window in windows:
        for core in range(cores):
            if window in target:
                pairs.append((index(window, core), index(target[window], core)))
            elif up:
                pairs.append((index(window, core), index(window, (core + 1) % cores)))
    return lax.ppermute(traces, ("sx", "sy", "core"), pairs)


def shards(op_real, op_imag, coef_right, coef_upper, sources):
    fields = sources[0, 0]
    _, count, rows = fields.shape
    right_coef = coef_right[0, 0]
    upper_coef = coef_upper[0, 0]
    rounds = lax.axis_size("sx") + lax.axis_size("sy") - 1
    own, own_hi, own_lo, other_hi, other_lo = start(fields, op_real[0, 0], op_imag[0, 0])
    traces = fields
    for turn in range(rounds):
        if turn:
            from_left = hand_over(traces, turn - 1, 1, 0)
            from_below = hand_over(traces, turn - 1, 0, 1)
            own = gather_chips(combine(fields, right_coef, upper_coef, from_left, from_below))
        other = lax.ppermute(own, "core", ring("core"))
        first = half_call(
            first_half_body, turn, (2 * count, 2 * rows), own, own_hi, own_lo, name="first_half"
        )
        traces = half_call(
            second_half_body, turn, fields.shape, other, other_hi, other_lo, first, traces,
            name="second_half",
        )
    return traces[None, None]


def solution(mesh):
    fine = Mesh(mesh.devices.reshape(4, 2, 4, 2, 2), ("sx", "sy", "y", "zl", "core"))
    op = ("y", "zl", "core")
    return jax.shard_map(
        shards,
        mesh=fine,
        in_specs=(
            P("sx", "sy", op, None),
            P("sx", "sy", op, None),
            P("sx", "sy", None, op),
            P("sx", "sy", None, op),
            P("sx", "sy", None, None, op),
        ),
        out_specs=P("sx", "sy", None, None, op),
        check_vma=False,
    )
```
